32 devices in a mesh: runs: 2 (over y), ctx: 4 (over z), head: 4 (over x, core).
Axes of the slice: x: 2, y: 2, z: 4, core: 2. Of those that a mesh axis runs over, the one named last changes fastest.
Arguments:
- tokens: bfloat16 [4096, 2048], P(('runs', 'ctx', 'head')), parts along dimension 0, may hold values from -400 to 400
- in_gain: float32 [2048], replicated, may hold values from 0.1 to 1.9
- projections: bfloat16 [3, 2048, 2048], P(None, 'ctx', 'head'), may hold values from -0.125 to 0.125
- prior_state: float32 [32, 128, 128], P(('runs', 'head')), parts along dimension 0, may hold values from -256 to 256
- out_gain: float32 [2048], P('head'), may hold values from 0.1 to 1.9
Outputs:
- attended: bfloat16 [4096, 2048], P(('runs', 'ctx', 'head')), parts along dimension 0
The draws below stay inside these ranges and needn't reach their ends.
There are 2 independent parts, one for each index of `runs`. The reference program is written for one: setup_inputs(seed, part) draws one part's arguments, and reference() takes and returns one part's arrays. A program takes and returns all parts, laid end to end along the dimension named above; an argument that names none is the same for every part. Nothing has to cross between parts.
All inputs are finite; a program needn't handle non-finite values.
Results may differ from the reference program's by a relative error of at most 0.0071.
Values may be sent and summed in bfloat16 or wider, within the bound.
A program may use at most 64 MiB of HBM per device.

```python
import math
import jax
import jax.numpy as jnp
from jax import lax

D = 2048
HEADS = 16
HEAD_DIM = 128
BLOCK = 512
SEQ = 2048


def draw_tokens(key, part):
    first, second, third = jax.random.split(key, 3)
    row_scale = jnp.exp(jax.random.uniform(first, (SEQ, 1), jnp.float32, 0.0, math.log(10.0)))
    col_scale = jnp.exp(jax.random.uniform(second, (1, D), jnp.float32, 0.0, math.log(10.0)))
    base = jnp.clip(jax.random.normal(third, (SEQ, D), jnp.float32), -4.0, 4.0)
    return (base * row_scale * col_scale).astype(jnp.bfloat16)


def steps_of(key, extent, pieces, least, top_value):
    level = 1.0
    for dim, blocks in pieces:
        heights = jax.random.uniform(jax.random.fold_in(jax.random.fold_in(key, 6), dim), (blocks,), jnp.float32, least / len(pieces), top_value / len(pieces))
        level = level * jnp.repeat(jnp.exp(heights), extent[dim] // blocks).reshape((-1,) + (1,) * (len(extent) - 1 - dim))
    return level


def gaussian(key, extent, scale, reach, cuts=(), kind=jnp.bfloat16):
    values = jax.random.normal(key, extent, jnp.float32) * scale
    if len(cuts) > 0:
        values = steps_of(key, extent, cuts, -0.22, 0.18) * values
    return jnp.clip(values, min=-reach, max=reach).astype(kind)


def setup_inputs(seed: int = 0, part: int = 0) -> dict:
    key_of = jax.random.split(jax.random.key(seed), 6)
    part_splits = jax.random.split(jax.random.fold_in(key_of[5], part), 6)
    return {
        "tokens": draw_tokens(jax.random.fold_in(jax.random.fold_in(key_of[5], part), 71), part),
        "in_gain": jnp.clip(1.0 + 0.18 * jax.random.normal(key_of[1], (D,), jnp.float32), 0.1, 1.9),
        "projections": gaussian(key_of[2], (3, D, D), D ** -0.5, 0.125, ((1, 4), (2, 4))),
        "prior_state": gaussian(part_splits[3], (HEADS, HEAD_DIM, HEAD_DIM), (SEQ ** 0.5), 256.0, ((0, 4),), jnp.float32),
        "out_gain": jnp.clip(1.0 + 0.18 * jax.random.normal(key_of[4], (D,), jnp.float32), 0.1, 1.9),
    }


def rms_tokens(values_in, gain):
    wide = values_in.astype(jnp.float32)
    scale = lax.rsqrt(lax.optimization_barrier(jnp.mean(wide * wide, axis=-1, keepdims=True)) + 1e-06)
    return (wide * scale * gain).astype(jnp.bfloat16)

def reference(tokens, in_gain, projections, prior_state, out_gain):
    normed = rms_tokens(tokens, in_gain)
    queries = jnp.dot(normed, projections[0], preferred_element_type=jnp.float32).astype(jnp.bfloat16)
    keys_all = jnp.dot(normed, projections[1], preferred_element_type=jnp.float32).astype(jnp.bfloat16)
    values_all = jnp.dot(normed, projections[2], preferred_element_type=jnp.float32).astype(jnp.bfloat16)
    count = SEQ // BLOCK
    queries = queries.reshape(count, BLOCK, HEADS, HEAD_DIM)
    keys_all = keys_all.reshape(count, BLOCK, HEADS, HEAD_DIM)
    values_all = values_all.reshape(count, BLOCK, HEADS, HEAD_DIM)
    position = jnp.arange(BLOCK, dtype=jnp.int32)
    causal = position[:, None] >= position[None, :]
    gains = out_gain.reshape(HEADS, HEAD_DIM)

    def advance(state, block_in):
        query_blk, key_blk, value_blk = block_in
        query_f = query_blk.astype(jnp.float32)
        key_f = key_blk.astype(jnp.float32)
        value_f = value_blk.astype(jnp.float32)
        scores = jnp.einsum('qhd,khd->hqk', query_f, key_f)
        scores = jnp.where(causal[None], scores, 0.0)
        rounded = lax.optimization_barrier(scores.astype(jnp.bfloat16)).astype(jnp.float32)
        intra = jnp.einsum('hqk,khd->qhd', rounded, value_f)
        state_low = lax.optimization_barrier(state.astype(jnp.bfloat16)).astype(jnp.float32)
        inter = jnp.einsum('qhd,hde->qhe', query_f, state_low)
        mixed = intra + inter
        scale = lax.rsqrt(lax.optimization_barrier(jnp.mean(mixed * mixed, axis=-1, keepdims=True)) + 1e-06)
        result = (mixed * scale * gains).astype(jnp.bfloat16).reshape(BLOCK, HEADS * HEAD_DIM)
        state = state + jnp.einsum('khd,khe->hde', key_f, value_f)
        return (state, result)
    _, outputs = lax.scan(advance, prior_state.astype(jnp.float32), (queries, keys_all, values_all))
    return outputs.reshape(SEQ, HEADS * HEAD_DIM)
```

```python
import functools

import jax
import jax.numpy as jnp
from jax import lax
from jax.experimental import pallas as pl
from jax.experimental.pallas import tpu as pltpu
from jax.sharding import PartitionSpec as P

BLOCK = 512
CORES = 2
MESH = pl.DeviceIdType.MESH
QUERY, KEY, VALUE = 0, 1, 2


def dot(a, b, contract=((1,), (0,))):
    return lax.dot_general(a, b, (contract, ((), ())), preferred_element_type=jnp.float32)


def kernel(
    n_ctx, n_head,
    tok_ref, gain_ref, w_ref, prior_ref, og_ref,
    out_ref,
    x_buf, w_buf, q_buf, k_buf, v_buf, att, sums, totals, others, starts,
    own_sem, tz_send, tz_recv, tx_send, tx_recv, tc_send, tc_recv,
    wz_send, wz_recv, wy_send, wy_recv, st_send, st_recv, o_send, o_recv, o_own,
):
    run = lax.axis_index("runs")
    z = lax.axis_index("ctx")
    h = lax.axis_index("head")
    n_x = n_head // CORES
    x, core = h // CORES, h % CORES
    half = z % 2
    partner = z + 1 - 2 * half
    rows_here = tok_ref.shape[0]
    rows = w_ref.shape[1]
    rows_half = rows // 2
    heads_here = prior_ref.shape[0]
    mine = heads_here // 2
    dim = prior_ref.shape[1]
    width = mine * dim
    n_tok = x_buf.shape[0]
    span = n_tok // 2
    n_blocks = n_tok // BLOCK
    n_pairs = n_ctx // 2
    other_run = {"runs": 1 - run}

    def slot(side, head):
        return pl.ds(pl.multiple_of((side * n_head + head) * rows_here, rows_here), rows_here)

    def cols(side):
        return pl.ds(pl.multiple_of(side * width, width), width)

    def w_rows(source, part):
        start = pl.multiple_of(source * rows + part * rows_half, rows_half)
        return pl.ds(start, rows_half)

    own_w = pltpu.make_async_copy(
        w_ref.at[:, :, cols(half)],
        w_buf.at[:, pl.ds(pl.multiple_of(z * rows, rows), rows), :],
        own_sem,
    )
    own_w.start()

    barrier = pltpu.get_barrier_semaphore()
    greeted = [other_run]
    greeted += [{"ctx": (z + k) % n_ctx} for k in range(1, n_ctx)]
    greeted += [{"head": (h + k) % n_head} for k in range(1, n_head)]
    greeted += [{"ctx": partner, "head": (h + k) % n_head} for k in range(1, n_head)]
    for device in greeted:
        pl.semaphore_signal(barrier, inc=1, device_id=device, device_id_type=MESH)

    wide = tok_ref[...].astype(jnp.float32)
    scale = lax.rsqrt(jnp.mean(wide * wide, axis=-1, keepdims=True) + 1e-06)
    x_buf[slot(half, h), :] = (wide * scale * gain_ref[...]).astype(jnp.bfloat16)
    pl.semaphore_wait(barrier, len(greeted))

    sent = []

    def send(src, dst, send_sem, recv_sem, device):
        copy = pltpu.make_async_remote_copy(
            src_ref=src, dst_ref=dst, send_sem=send_sem, recv_sem=recv_sem,
            device_id=device, device_id_type=MESH,
        )
        copy.start()
        sent.append(copy)

    def arrived(dst, send_sem, recv_sem):
        pltpu.make_async_remote_copy(
            src_ref=dst, dst_ref=dst, send_sem=send_sem, recv_sem=recv_sem,
            device_id=other_run, device_id_type=MESH,
        ).wait_recv()

    def spread(side, b):
        block = x_buf.at[slot(side, h), :]
        for d in range(1, n_x):
            send(block, block, tx_send.at[d, b], tx_recv.at[d, b],
                 {"head": ((x + d) % n_x) * CORES + core})
        send(block, block, tc_send.at[0, b], tc_recv.at[0, b],
             {"head": x * CORES + 1 - core})

    def pass_on(side, b):
        for d in range(1, n_x):
            head = ((x + n_x - d) % n_x) * CORES + core
            block = x_buf.at[slot(side, head), :]
            arrived(block, tx_send.at[d, b], tx_recv.at[d, b])
            send(block, block, tc_send.at[d, b], tc_recv.at[d, b],
                 {"head": x * CORES + 1 - core})

    def send_weights(j):
        for k in range(1, n_ctx):
            to = (z + k) % n_ctx
            part = pl.ds(pl.multiple_of(run * rows_half, rows_half), rows_half)
            send(w_ref.at[j, part, cols(to % 2)], w_buf.at[j, w_rows(z, run), :],
                 wz_send.at[j, k], wz_recv.at[j, k], {"ctx": to})

    def swap_weights(j):
        for k in range(1, n_ctx):
            piece = w_buf.at[j, w_rows((z + n_ctx - k) % n_ctx, run), :]
            arrived(piece, wz_send.at[j, k], wz_recv.at[j, k])
            send(piece, piece, wy_send.at[j, k], wy_recv.at[j, k], other_run)

    def wait_weights(j):
        for k in range(1, n_ctx):
            piece = w_buf.at[j, w_rows((z + n_ctx - k) % n_ctx, 1 - run), :]
            arrived(piece, wy_send.at[j, k], wy_recv.at[j, k])

    def project(j, to):
        def tile(step, carry):
            at = pl.ds(pl.multiple_of(step * 256, 256), 256)
            to[at, :] = dot(x_buf[at, :], w_buf[j]).astype(jnp.bfloat16)
            return carry

        lax.fori_loop(0, n_tok // 256, tile, 0)

    block = x_buf.at[slot(half, h), :]
    send(block, block, tz_send, tz_recv, {"ctx": partner})
    spread(half, 0)
    send_weights(KEY)
    send_weights(VALUE)
    send_weights(QUERY)
    arrived(x_buf.at[slot(1 - half, h), :], tz_send, tz_recv)
    spread(1 - half, 1)
    pass_on(half, 0)
    swap_weights(KEY)
    pass_on(1 - half, 1)
    swap_weights(VALUE)
    for d in range(n_x):
        head = ((x + n_x - d) % n_x) * CORES + 1 - core
        for b, side in ((0, half), (1, 1 - half)):
            arrived(x_buf.at[slot(side, head), :], tc_send.at[d, b], tc_recv.at[d, b])
    own_w.wait()
    wait_weights(KEY)
    project(KEY, k_buf)
    swap_weights(QUERY)
    wait_weights(VALUE)
    project(VALUE, v_buf)

    for i in range(mine):
        at = pl.ds(i * dim, dim)
        total = None
        for b in range(n_blocks):
            here = pl.ds(b * BLOCK, BLOCK)
            one = dot(k_buf[here, at], v_buf[here, at], ((0,), (0,)))
            sums[b, i] = one
            total = one if total is None else total + one
        totals[i] = total
    for k in range(1, n_pairs):
        send(totals, others.at[k], st_send.at[k], st_recv.at[k], {"ctx": (z + 2 * k) % n_ctx})

    wait_weights(QUERY)
    project(QUERY, q_buf)

    for k in range(1, n_pairs):
        arrived(others.at[k], st_send.at[k], st_recv.at[k])
    for i in range(mine):
        state = prior_ref[half * mine + i]
        for k in range(1, n_pairs):
            state = state + jnp.where(z >= 2 * k, others[k, i], 0.0)
        for b in range(n_blocks):
            starts[b, i] = state.astype(jnp.bfloat16)
            state = state + sums[b, i]

    step_rows = 256
    out_cols = pl.ds(pl.multiple_of((h * 2 + half) * width, width), width)
    per_span = span // BLOCK
    for dz in (1, 0):
        side = (half + dz) % 2
        for bb in range(per_span):
            b = side * per_span + bb
            base = pl.multiple_of(b * BLOCK, BLOCK)
            for i in range(mine):
                at = pl.ds(i * dim, dim)
                gains = og_ref[half * mine + i]
                start = starts[b, i]
                for r in range(0, BLOCK, step_rows):
                    seen = r + step_rows
                    here = pl.ds(pl.multiple_of(base + r, step_rows), step_rows)
                    query = q_buf[here, at]
                    before = pl.ds(base, seen)
                    scores = dot(query, k_buf[before, at], ((1,), (1,)))
                    row = lax.broadcasted_iota(jnp.int32, (step_rows, seen), 0) + r
                    col = lax.broadcasted_iota(jnp.int32, (step_rows, seen), 1)
                    scores = jnp.where(row >= col, scores, 0.0).astype(jnp.bfloat16)
                    mixed = dot(scores, v_buf[before, at]) + dot(query, start)
                    level = lax.rsqrt(jnp.mean(mixed * mixed, axis=-1, keepdims=True) + 1e-06)
                    att[here, at] = (mixed * level * gains).astype(jnp.bfloat16)
        for dh in range(n_head):
            if dz == 0 and dh == 0:
                continue
            head = (h + dh) % n_head
            send(att.at[slot(side, head), :], out_ref.at[:, out_cols],
                 o_send.at[dz, dh], o_recv.at[dz, dh],
                 {"ctx": z + side - half, "head": head})
    own_out = pltpu.make_async_copy(att.at[slot(half, h), :], out_ref.at[:, out_cols], o_own)
    own_out.start()
    own_out.wait()
    for dz in (1, 0):
        for dh in range(n_head):
            if dz == 0 and dh == 0:
                continue
            source = ((h + n_head - dh) % n_head) * 2 + (half + dz) % 2
            place = pl.ds(pl.multiple_of(source * width, width), width)
            arrived(out_ref.at[:, place], o_send.at[dz, dh], o_recv.at[dz, dh])
    for copy in sent:
        copy.wait_send()


def on_device(n_ctx, n_head, tokens, in_gain, projections, prior_state, out_gain):
    rows_here, features = tokens.shape
    heads_here, dim, _ = prior_state.shape
    mine = heads_here // 2
    width = mine * dim
    n_tok = 2 * n_head * rows_here
    n_blocks = n_tok // BLOCK
    n_x = n_head // CORES
    dma = pltpu.SemaphoreType.DMA
    vmem = pl.BlockSpec(memory_space=pltpu.VMEM)
    bf16, f32 = jnp.bfloat16, jnp.float32
    return pl.pallas_call(
        functools.partial(kernel, n_ctx, n_head),
        out_shape=jax.ShapeDtypeStruct((rows_here, features), bf16),
        in_specs=[vmem, vmem, pl.BlockSpec(memory_space=pl.ANY), vmem, vmem],
        out_specs=vmem,
        scratch_shapes=[
            pltpu.VMEM((n_tok, features), bf16),
            pltpu.VMEM((3, features, width), bf16),
            pltpu.VMEM((n_tok, width), bf16),
            pltpu.VMEM((n_tok, width), bf16),
            pltpu.VMEM((n_tok, width), bf16),
            pltpu.VMEM((n_tok, width), bf16),
            pltpu.VMEM((n_blocks, mine, dim, dim), f32),
            pltpu.VMEM((mine, dim, dim), f32),
            pltpu.VMEM((n_ctx // 2, mine, dim, dim), f32),
            pltpu.VMEM((n_blocks, mine, dim, dim), bf16),
            dma, dma, dma,
            dma((n_x, 2)), dma((n_x, 2)), dma((n_x, 2)), dma((n_x, 2)),
            dma((3, n_ctx)), dma((3, n_ctx)), dma((3, n_ctx)), dma((3, n_ctx)),
            dma((n_ctx // 2,)), dma((n_ctx // 2,)),
            dma((2, n_head)), dma((2, n_head)), dma,
        ],
        compiler_params=pltpu.CompilerParams(
            collective_id=0, has_side_effects=True, vmem_limit_bytes=50 * 1024 * 1024
        ),
    )(
        tokens,
        in_gain.reshape(1, features),
        projections,
        prior_state,
        out_gain.reshape(heads_here, 1, dim),
    )


def solution(mesh):
    in_specs = (
        P(("runs", "ctx", "head"), None),
        P(),
        P(None, "ctx", "head"),
        P(("runs", "head"), None, None),
        P("head"),
    )
    out_specs = P(("runs", "ctx", "head"), None)
    return jax.shard_map(
        functools.partial(on_device, mesh.shape["ctx"], mesh.shape["head"]),
        mesh=mesh, in_specs=in_specs, out_specs=out_specs, check_vma=False,
    )
```

```python
import functools

import jax
import jax.numpy as jnp
from jax import lax
from jax.experimental import pallas as pl
from jax.experimental.pallas import tpu as pltpu
from jax.sharding import PartitionSpec as P

BLOCK = 512
CORES = 2
MESH = pl.DeviceIdType.MESH
QUERY, KEY, VALUE = 0, 1, 2
AHEAD = 6
AT_PARTNER, AT_FIRST, AT_SECOND, AT_KEYS, AT_VALUES = 2, 3, 7, 11, 12


def dot(a, b, contract=((1,), (0,))):
    return lax.dot_general(a, b, (contract, ((), ())), preferred_element_type=jnp.float32)


def kernel(
    n_ctx, n_head,
    tok_hbm, gain_hbm, w_ref, prior_hbm, og_hbm,
    out_ref,
    tok_ref, gain_ref, prior_ref, og_ref, in_sems,
    x_buf, w_buf, q_buf, k_buf, v_buf, att, sums, totals, others, starts,
    own_sem, tz_send, tz_recv, tx_send, tx_recv, tc_send, tc_recv,
    wz_send, wz_recv, wy_send, wy_recv, st_send, st_recv, oz_send, oz_recv, o_send, o_recv, o_own,
):
    run = lax.axis_index("runs")
    z = lax.axis_index("ctx")
    h = lax.axis_index("head")
    n_x = n_head // CORES
    x, core = h // CORES, h % CORES
    half = z % 2
    partner = z + 1 - 2 * half
    rows_here = tok_ref.shape[0]
    rows = w_ref.shape[1]
    rows_half = rows // 2
    cuts = wz_send.shape[0] // 3
    rows_cut = rows_half // cuts
    stages = [(j, cut) for j in (KEY, VALUE, QUERY) for cut in range(cuts)]
    mine = prior_ref.shape[0]
    dim = prior_ref.shape[1]
    width = mine * dim
    n_tok = x_buf.shape[0]
    span = n_tok // 2
    n_blocks = n_tok // BLOCK
    n_pairs = n_ctx // 2
    other_run = {"runs": 1 - run}

    def slot(side, head):
        return pl.ds(pl.multiple_of((side * n_head + head) * rows_here, rows_here), rows_here)

    def cols(side):
        return pl.ds(pl.multiple_of(side * width, width), width)

    def w_rows(source, part, cut):
        start = pl.multiple_of(source * rows + part * rows_half + cut * rows_cut, rows_cut)
        return pl.ds(start, rows_cut)

    own_w = pltpu.make_async_copy(
        w_ref.at[:, :, cols(half)],
        w_buf.at[:, pl.ds(pl.multiple_of(z * rows, rows), rows), :],
        own_sem,
    )
    my_heads = pl.ds(half * mine, mine)
    loads = [
        pltpu.make_async_copy(src, dst, in_sems.at[n])
        for n, (src, dst) in enumerate((
            (tok_hbm, tok_ref), (gain_hbm, gain_ref),
            (prior_hbm.at[my_heads], prior_ref), (og_hbm.at[my_heads], og_ref),
        ))
    ]
    for load in loads:
        load.start()
    own_w.start()

    barrier = pltpu.get_barrier_semaphore()
    greeted = [other_run]
    greeted += [{"ctx": (z + k) % n_ctx} for k in range(1, n_ctx)]
    greeted += [{"head": (h + k) % n_head} for k in range(1, n_head)]
    greeted += [{"ctx": partner, "head": (h + k) % n_head} for k in range(1, n_head)]
    for device in greeted:
        pl.semaphore_signal(barrier, inc=1, device_id=device, device_id_type=MESH)

    loads[0].wait()
    loads[1].wait()
    wide = tok_ref[...].astype(jnp.float32)
    scale = lax.rsqrt(jnp.mean(wide * wide, axis=-1, keepdims=True) + 1e-06)
    x_buf[slot(half, h), :] = (wide * scale * gain_ref[...]).astype(jnp.bfloat16)
    pl.semaphore_wait(barrier, len(greeted))

    sent = []

    def send(src, dst, send_sem, recv_sem, device):
        copy = pltpu.make_async_remote_copy(
            src_ref=src, dst_ref=dst, send_sem=send_sem, recv_sem=recv_sem,
            device_id=device, device_id_type=MESH,
        )
        copy.start()
        sent.append(copy)

    def arrived(dst, send_sem, recv_sem):
        pltpu.make_async_remote_copy(
            src_ref=dst, dst_ref=dst, send_sem=send_sem, recv_sem=recv_sem,
            device_id=other_run, device_id_type=MESH,
        ).wait_recv()

    def spread(side, b):
        block = x_buf.at[slot(side, h), :]
        for d in range(1, n_x):
            send(block, block, tx_send.at[d, b], tx_recv.at[d, b],
                 {"head": ((x + d) % n_x) * CORES + core})
        send(block, block, tc_send.at[0, b], tc_recv.at[0, b],
             {"head": x * CORES + 1 - core})

    def pass_on(side, b):
        for d in range(1, n_x):
            head = ((x + n_x - d) % n_x) * CORES + core
            block = x_buf.at[slot(side, head), :]
            arrived(block, tx_send.at[d, b], tx_recv.at[d, b])
            send(block, block, tc_send.at[d, b], tc_recv.at[d, b],
                 {"head": x * CORES + 1 - core})

    def send_weights(stage):
        j, cut = stages[stage]
        for k in range(1, n_ctx):
            to = (z + k) % n_ctx
            start = pl.multiple_of(run * rows_half + cut * rows_cut, rows_cut)
            send(w_ref.at[j, pl.ds(start, rows_cut), cols(to % 2)],
                 w_buf.at[j, w_rows(z, run, cut), :],
                 wz_send.at[stage, k], wz_recv.at[stage, k], {"ctx": to})

    def swap_weights(stage):
        j, cut = stages[stage]
        for k in range(1, n_ctx):
            piece = w_buf.at[j, w_rows((z + n_ctx - k) % n_ctx, run, cut), :]
            arrived(piece, wz_send.at[stage, k], wz_recv.at[stage, k])
            send(piece, piece, wy_send.at[stage, k], wy_recv.at[stage, k], other_run)

    def wait_weights(matrix):
        for stage, (j, cut) in enumerate(stages):
            if j != matrix:
                continue
            for k in range(1, n_ctx):
                piece = w_buf.at[j, w_rows((z + n_ctx - k) % n_ctx, 1 - run, cut), :]
                arrived(piece, wy_send.at[stage, k], wy_recv.at[stage, k])

    def project(j, to):
        def tile(step, carry):
            at = pl.ds(pl.multiple_of(step * 256, 256), 256)
            to[at, :] = dot(x_buf[at, :], w_buf[j]).astype(jnp.bfloat16)
            return carry

        lax.fori_loop(0, n_tok // 256, tile, 0)

    def start_tokens():
        block = x_buf.at[slot(half, h), :]
        send(block, block, tz_send, tz_recv, {"ctx": partner})
        spread(half, 0)

    def partner_tokens():
        arrived(x_buf.at[slot(1 - half, h), :], tz_send, tz_recv)
        spread(1 - half, 1)

    def wait_tokens():
        for d in range(n_x):
            head = ((x + n_x - d) % n_x) * CORES + 1 - core
            for b, side in ((0, half), (1, 1 - half)):
                arrived(x_buf.at[slot(side, head), :], tc_send.at[d, b], tc_recv.at[d, b])

    def do_keys():
        wait_weights(KEY)
        project(KEY, k_buf)

    def do_values():
        wait_weights(VALUE)
        project(VALUE, v_buf)

    def do_sums():
        for i in range(mine):
            at = pl.ds(i * dim, dim)
            total = None
            for b in range(n_blocks):
                here = pl.ds(b * BLOCK, BLOCK)
                one = dot(k_buf[here, at], v_buf[here, at], ((0,), (0,)))
                sums[b, i] = one
                total = one if total is None else total + one
            totals[i] = total
        for k in range(1, n_pairs):
            send(totals, others.at[k], st_send.at[k], st_recv.at[k],
                 {"ctx": (z + 2 * k) % n_ctx})

    def do_starts():
        for k in range(1, n_pairs):
            arrived(others.at[k], st_send.at[k], st_recv.at[k])
        for i in range(mine):
            state = prior_ref[i]
            for k in range(1, n_pairs):
                state = state + jnp.where(z >= 2 * k, others[k, i], 0.0)
            for b in range(n_blocks):
                starts[b, i] = state.astype(jnp.bfloat16)
                state = state + sums[b, i]

    n_stages = len(stages)
    ahead = min(AHEAD * cuts // 4, n_stages)
    between = [[] for _ in range(n_stages + 1)]
    for at, work in (
        (AT_PARTNER, (partner_tokens,)),
        (AT_FIRST, (functools.partial(pass_on, half, 0),)),
        (AT_SECOND, (functools.partial(pass_on, 1 - half, 1),)),
        (AT_KEYS, (wait_tokens, own_w.wait, loads[2].wait, loads[3].wait, do_keys)),
        (AT_VALUES, (do_values, do_sums)),
    ):
        between[at * cuts // 4] += work
    start_tokens()
    for stage in range(ahead):
        send_weights(stage)
    for stage in range(n_stages):
        for work in between[stage]:
            work()
        swap_weights(stage)
        if stage + ahead < n_stages:
            send_weights(stage + ahead)
    for work in between[n_stages]:
        work()
    do_starts()
    wait_weights(QUERY)
    project(QUERY, q_buf)

    step_rows = 256
    out_cols = pl.ds(pl.multiple_of((h * 2 + half) * width, width), width)
    per_span = span // BLOCK

    def attend(side, bb, r):
        b = side * per_span + bb
        base = pl.multiple_of(b * BLOCK, BLOCK)
        seen = r + step_rows
        here = pl.ds(pl.multiple_of(base + r, step_rows), step_rows)
        before = pl.ds(base, seen)
        row = lax.broadcasted_iota(jnp.int32, (step_rows, seen), 0) + r
        col = lax.broadcasted_iota(jnp.int32, (step_rows, seen), 1)
        for i in range(mine):
            at = pl.ds(i * dim, dim)
            query = q_buf[here, at]
            scores = dot(query, k_buf[before, at], ((1,), (1,)))
            scores = jnp.where(row >= col, scores, 0.0).astype(jnp.bfloat16)
            mixed = dot(scores, v_buf[before, at]) + dot(query, starts[b, i])
            level = lax.rsqrt(jnp.mean(mixed * mixed, axis=-1, keepdims=True) + 1e-06)
            att[here, at] = (mixed * level * og_ref[i]).astype(jnp.bfloat16)

    for bb in range(per_span):
        for r in range(0, BLOCK, step_rows):
            attend(1 - half, bb, r)
            first = (bb * BLOCK + r) // rows_here
            for head in range(first, first + step_rows // rows_here):
                send(att.at[slot(1 - half, head), :], out_ref.at[:, out_cols],
                     oz_send.at[head], oz_recv.at[h], {"ctx": partner, "head": head})
    for bb in range(per_span):
        for r in range(0, BLOCK, step_rows):
            attend(half, bb, r)
    for dh in range(1, n_head):
        send(att.at[slot(half, (h + dh) % n_head), :], out_ref.at[:, out_cols],
             o_send.at[dh], o_recv.at[dh], {"head": (h + dh) % n_head})
    own_out = pltpu.make_async_copy(att.at[slot(half, h), :], out_ref.at[:, out_cols], o_own)
    own_out.start()

    def out_place(head, side):
        return out_ref.at[:, pl.ds(pl.multiple_of((head * 2 + side) * width, width), width)]

    for head in range(n_head):
        arrived(out_place(head, 1 - half), oz_send.at[head], oz_recv.at[head])
    for dh in range(1, n_head):
        arrived(out_place((h + n_head - dh) % n_head, half), o_send.at[dh], o_recv.at[dh])
    own_out.wait()
    for copy in sent:
        copy.wait_send()


def on_device(n_ctx, n_head, tokens, in_gain, projections, prior_state, out_gain):
    rows_here, features = tokens.shape
    heads_here, dim, _ = prior_state.shape
    mine = heads_here // 2
    width = mine * dim
    n_tok = 2 * n_head * rows_here
    n_blocks = n_tok // BLOCK
    n_x = n_head // CORES
    cuts = min(4, projections.shape[1] // 32)
    dma = pltpu.SemaphoreType.DMA
    vmem = pl.BlockSpec(memory_space=pltpu.VMEM)
    bf16, f32 = jnp.bfloat16, jnp.float32
    return pl.pallas_call(
        functools.partial(kernel, n_ctx, n_head),
        out_shape=jax.ShapeDtypeStruct((rows_here, features), bf16),
        in_specs=[pl.BlockSpec(memory_space=pltpu.HBM)] * 5,
        out_specs=vmem,
        scratch_shapes=[
            pltpu.VMEM((rows_here, features), bf16),
            pltpu.VMEM((1, features), f32),
            pltpu.VMEM((mine, dim, dim), f32),
            pltpu.VMEM((mine, 1, dim), f32),
            dma((4,)),
            pltpu.VMEM((n_tok, features), bf16),
            pltpu.VMEM((3, features, width), bf16),
            pltpu.VMEM((n_tok, width), bf16),
            pltpu.VMEM((n_tok, width), bf16),
            pltpu.VMEM((n_tok, width), bf16),
            pltpu.VMEM((n_tok, width), bf16),
            pltpu.VMEM((n_blocks, mine, dim, dim), f32),
            pltpu.VMEM((mine, dim, dim), f32),
            pltpu.VMEM((n_ctx // 2, mine, dim, dim), f32),
            pltpu.VMEM((n_blocks, mine, dim, dim), bf16),
            dma, dma, dma,
            dma((n_x, 2)), dma((n_x, 2)), dma((n_x, 2)), dma((n_x, 2)),
            dma((3 * cuts, n_ctx)), dma((3 * cuts, n_ctx)),
            dma((3 * cuts, n_ctx)), dma((3 * cuts, n_ctx)),
            dma((n_ctx // 2,)), dma((n_ctx // 2,)),
            dma((n_head,)), dma((n_head,)), dma((n_head,)), dma((n_head,)), dma,
        ],
        compiler_params=pltpu.CompilerParams(
            collective_id=0, has_side_effects=True, vmem_limit_bytes=60 * 1024 * 1024
        ),
    )(
        tokens,
        in_gain.reshape(1, features),
        projections,
        prior_state,
        out_gain.reshape(heads_here, 1, dim),
    )


def solution(mesh):
    in_specs = (
        P(("runs", "ctx", "head"), None),
        P(),
        P(None, "ctx", "head"),
        P(("runs", "head"), None, None),
        P("head"),
    )
    out_specs = P(("runs", "ctx", "head"), None)
    return jax.shard_map(
        functools.partial(on_device, mesh.shape["ctx"], mesh.shape["head"]),
        mesh=mesh, in_specs=in_specs, out_specs=out_specs, check_vma=False,
    )
```

```python
import functools

import jax
import jax.numpy as jnp
from jax import lax
from jax.experimental import pallas as pl
from jax.experimental.pallas import tpu as pltpu
from jax.sharding import PartitionSpec as P

BLOCK = 512
CORES = 2
MESH = pl.DeviceIdType.MESH
QUERY, KEY, VALUE = 0, 1, 2
AHEAD = 6
AT_PARTNER, AT_FIRST, AT_SECOND, AT_KEYS, AT_VALUES = 2, 3, 9, 10, 11


def dot(a, b, contract=((1,), (0,))):
    return lax.dot_general(a, b, (contract, ((), ())), preferred_element_type=jnp.float32)


def kernel(
    n_ctx, n_head,
    tok_hbm, gain_hbm, w_ref, prior_hbm, og_hbm,
    out_ref,
    tok_ref, gain_ref, prior_ref, og_ref, in_sems,
    x_buf, w_buf, q_buf, k_buf, v_buf, att, sums, totals, others, starts,
    own_sem, tz_send, tz_recv, tx_send, tx_recv, tc_send, tc_recv,
    wz_send, wz_recv, wy_send, wy_recv, st_send, st_recv, oz_send, oz_recv, o_send, o_recv, o_own,
):
    run = lax.axis_index("runs")
    z = lax.axis_index("ctx")
    h = lax.axis_index("head")
    n_x = n_head // CORES
    x, core = h // CORES, h % CORES
    half = z % 2
    partner = z + 1 - 2 * half
    rows_here = tok_ref.shape[0]
    rows = w_ref.shape[1]
    rows_half = rows // 2
    cuts = wz_send.shape[0] // 3
    rows_cut = rows_half // cuts
    stages = [(j, cut) for j in (KEY, VALUE, QUERY) for cut in range(cuts)]
    mine = prior_ref.shape[0]
    dim = prior_ref.shape[1]
    width = mine * dim
    n_tok = x_buf.shape[0]
    span = n_tok // 2
    n_blocks = n_tok // BLOCK
    n_pairs = n_ctx // 2
    other_run = {"runs": 1 - run}

    def slot(side, head):
        return pl.ds(pl.multiple_of((side * n_head + head) * rows_here, rows_here), rows_here)

    def cols(side):
        return pl.ds(pl.multiple_of(side * width, width), width)

    def w_rows(source, part, cut):
        start = pl.multiple_of(source * rows + part * rows_half + cut * rows_cut, rows_cut)
        return pl.ds(start, rows_cut)

    own_w = pltpu.make_async_copy(
        w_ref.at[:, :, cols(half)],
        w_buf.at[:, pl.ds(pl.multiple_of(z * rows, rows), rows), :],
        own_sem,
    )
    my_heads = pl.ds(half * mine, mine)
    loads = [
        pltpu.make_async_copy(src, dst, in_sems.at[n])
        for n, (src, dst) in enumerate((
            (tok_hbm, tok_ref), (gain_hbm, gain_ref),
            (prior_hbm.at[my_heads], prior_ref), (og_hbm.at[my_heads], og_ref),
        ))
    ]
    for load in loads:
        load.start()
    own_w.start()

    barrier = pltpu.get_barrier_semaphore()
    greeted = [other_run]
    greeted += [{"ctx": (z + k) % n_ctx} for k in range(1, n_ctx)]
    greeted += [{"head": (h + k) % n_head} for k in range(1, n_head)]
    greeted += [{"ctx": partner, "head": (h + k) % n_head} for k in range(1, n_head)]
    for device in greeted:
        pl.semaphore_signal(barrier, inc=1, device_id=device, device_id_type=MESH)

    loads[0].wait()
    loads[1].wait()
    wide = tok_ref[...].astype(jnp.float32)
    scale = lax.rsqrt(jnp.mean(wide * wide, axis=-1, keepdims=True) + 1e-06)
    x_buf[slot(half, h), :] = (wide * scale * gain_ref[...]).astype(jnp.bfloat16)
    pl.semaphore_wait(barrier, len(greeted))

    sent = []

    def send(src, dst, send_sem, recv_sem, device):
        copy = pltpu.make_async_remote_copy(
            src_ref=src, dst_ref=dst, send_sem=send_sem, recv_sem=recv_sem,
            device_id=device, device_id_type=MESH,
        )
        copy.start()
        sent.append(copy)

    def arrived(dst, send_sem, recv_sem):
        pltpu.make_async_remote_copy(
            src_ref=dst, dst_ref=dst, send_sem=send_sem, recv_sem=recv_sem,
            device_id=other_run, device_id_type=MESH,
        ).wait_recv()

    def spread(side, b):
        block = x_buf.at[slot(side, h), :]
        for d in range(1, n_x):
            send(block, block, tx_send.at[d, b], tx_recv.at[d, b],
                 {"head": ((x + d) % n_x) * CORES + core})
        send(block, block, tc_send.at[0, b], tc_recv.at[0, b],
             {"head": x * CORES + 1 - core})

    def pass_on(side, b):
        for d in range(1, n_x):
            head = ((x + n_x - d) % n_x) * CORES + core
            block = x_buf.at[slot(side, head), :]
            arrived(block, tx_send.at[d, b], tx_recv.at[d, b])
            send(block, block, tc_send.at[d, b], tc_recv.at[d, b],
                 {"head": x * CORES + 1 - core})

    def send_weights(stage):
        j, cut = stages[stage]
        for k in range(1, n_ctx):
            to = (z + k) % n_ctx
            start = pl.multiple_of(run * rows_half + cut * rows_cut, rows_cut)
            send(w_ref.at[j, pl.ds(start, rows_cut), cols(to % 2)],
                 w_buf.at[j, w_rows(z, run, cut), :],
                 wz_send.at[stage, k], wz_recv.at[stage, k], {"ctx": to})

    def swap_weights(stage):
        j, cut = stages[stage]
        for k in range(1, n_ctx):
            piece = w_buf.at[j, w_rows((z + n_ctx - k) % n_ctx, run, cut), :]
            arrived(piece, wz_send.at[stage, k], wz_recv.at[stage, k])
            send(piece, piece, wy_send.at[stage, k], wy_recv.at[stage, k], other_run)

    def wait_weights(matrix):
        for stage, (j, cut) in enumerate(stages):
            if j != matrix:
                continue
            for k in range(1, n_ctx):
                piece = w_buf.at[j, w_rows((z + n_ctx - k) % n_ctx, 1 - run, cut), :]
                arrived(piece, wy_send.at[stage, k], wy_recv.at[stage, k])

    def project(j, to):
        def tile(step, carry):
            at = pl.ds(pl.multiple_of(step * 256, 256), 256)
            to[at, :] = dot(x_buf[at, :], w_buf[j]).astype(jnp.bfloat16)
            return carry

        lax.fori_loop(0, n_tok // 256, tile, 0)

    def start_tokens():
        block = x_buf.at[slot(half, h), :]
        send(block, block, tz_send, tz_recv, {"ctx": partner})
        spread(half, 0)

    def partner_tokens():
        arrived(x_buf.at[slot(1 - half, h), :], tz_send, tz_recv)
        spread(1 - half, 1)

    def wait_tokens():
        for d in range(n_x):
            head = ((x + n_x - d) % n_x) * CORES + 1 - core
            for b, side in ((0, half), (1, 1 - half)):
                arrived(x_buf.at[slot(side, head), :], tc_send.at[d, b], tc_recv.at[d, b])

    def do_keys():
        wait_weights(KEY)
        project(KEY, k_buf)

    def do_values():
        wait_weights(VALUE)
        project(VALUE, v_buf)

    def do_sums():
        for i in range(mine):
            at = pl.ds(i * dim, dim)
            total = None
            for b in range(n_blocks):
                here = pl.ds(b * BLOCK, BLOCK)
                one = dot(k_buf[here, at], v_buf[here, at], ((0,), (0,)))
                sums[b, i] = one
                total = one if total is None else total + one
            totals[i] = total
        for k in range(1, n_pairs):
            send(totals, others.at[k], st_send.at[k], st_recv.at[k],
                 {"ctx": (z + 2 * k) % n_ctx})

    def do_starts():
        for k in range(1, n_pairs):
            arrived(others.at[k], st_send.at[k], st_recv.at[k])
        for i in range(mine):
            state = prior_ref[i]
            for k in range(1, n_pairs):
                state = state + jnp.where(z >= 2 * k, others[k, i], 0.0)
            for b in range(n_blocks):
                starts[b, i] = state.astype(jnp.bfloat16)
                state = state + sums[b, i]

    n_stages = len(stages)
    ahead = min(AHEAD * cuts // 4, n_stages)
    between = [[] for _ in range(n_stages + 1)]
    for at, work in (
        (AT_PARTNER, (partner_tokens,)),
        (AT_FIRST, (functools.partial(pass_on, half, 0),)),
        (AT_SECOND, (functools.partial(pass_on, 1 - half, 1),)),
        (AT_KEYS, (wait_tokens, own_w.wait, loads[2].wait, loads[3].wait, do_keys)),
        (AT_VALUES, (do_values, do_sums)),
    ):
        between[at * cuts // 4] += work
    start_tokens()
    for stage in range(ahead):
        send_weights(stage)
    for stage in range(n_stages):
        for work in between[stage]:
            work()
        swap_weights(stage)
        if stage + ahead < n_stages:
            send_weights(stage + ahead)
    for work in between[n_stages]:
        work()
    do_starts()
    wait_weights(QUERY)

    step_rows = 256
    out_cols = pl.ds(pl.multiple_of((h * 2 + half) * width, width), width)
    per_span = span // BLOCK

    def attend(side, bb, r):
        b = side * per_span + bb
        base = pl.multiple_of(b * BLOCK, BLOCK)
        seen = r + step_rows
        here = pl.ds(pl.multiple_of(base + r, step_rows), step_rows)
        before = pl.ds(base, seen)
        q_buf[here, :] = dot(x_buf[here, :], w_buf[QUERY]).astype(jnp.bfloat16)
        row = lax.broadcasted_iota(jnp.int32, (step_rows, seen), 0) + r
        col = lax.broadcasted_iota(jnp.int32, (step_rows, seen), 1)
        for i in range(mine):
            at = pl.ds(i * dim, dim)
            query = q_buf[here, at]
            scores = dot(query, k_buf[before, at], ((1,), (1,)))
            scores = jnp.where(row >= col, scores, 0.0).astype(jnp.bfloat16)
            mixed = dot(scores, v_buf[before, at]) + dot(query, starts[b, i])
            level = lax.rsqrt(jnp.mean(mixed * mixed, axis=-1, keepdims=True) + 1e-06)
            att[here, at] = (mixed * level * og_ref[i]).astype(jnp.bfloat16)

    for bb in range(per_span):
        for r in range(0, BLOCK, step_rows):
            attend(1 - half, bb, r)
            first = (bb * BLOCK + r) // rows_here
            for head in range(first, first + step_rows // rows_here):
                send(att.at[slot(1 - half, head), :], out_ref.at[:, out_cols],
                     oz_send.at[head], oz_recv.at[h], {"ctx": partner, "head": head})
    for bb in range(per_span):
        for r in range(0, BLOCK, step_rows):
            attend(half, bb, r)
    for dh in range(1, n_head):
        send(att.at[slot(half, (h + dh) % n_head), :], out_ref.at[:, out_cols],
             o_send.at[dh], o_recv.at[dh], {"head": (h + dh) % n_head})
    own_out = pltpu.make_async_copy(att.at[slot(half, h), :], out_ref.at[:, out_cols], o_own)
    own_out.start()

    def out_place(head, side):
        return out_ref.at[:, pl.ds(pl.multiple_of((head * 2 + side) * width, width), width)]

    for head in range(n_head):
        arrived(out_place(head, 1 - half), oz_send.at[head], oz_recv.at[head])
    for dh in range(1, n_head):
        arrived(out_place((h + n_head - dh) % n_head, half), o_send.at[dh], o_recv.at[dh])
    own_out.wait()
    for copy in sent:
        copy.wait_send()


def on_device(n_ctx, n_head, tokens, in_gain, projections, prior_state, out_gain):
    rows_here, features = tokens.shape
    heads_here, dim, _ = prior_state.shape
    mine = heads_here // 2
    width = mine * dim
    n_tok = 2 * n_head * rows_here
    n_blocks = n_tok // BLOCK
    n_x = n_head // CORES
    cuts = min(4, projections.shape[1] // 32)
    dma = pltpu.SemaphoreType.DMA
    vmem = pl.BlockSpec(memory_space=pltpu.VMEM)
    bf16, f32 = jnp.bfloat16, jnp.float32
    return pl.pallas_call(
        functools.partial(kernel, n_ctx, n_head),
        out_shape=jax.ShapeDtypeStruct((rows_here, features), bf16),
        in_specs=[pl.BlockSpec(memory_space=pltpu.HBM)] * 5,
        out_specs=vmem,
        scratch_shapes=[
            pltpu.VMEM((rows_here, features), bf16),
            pltpu.VMEM((1, features), f32),
            pltpu.VMEM((mine, dim, dim), f32),
            pltpu.VMEM((mine, 1, dim), f32),
            dma((4,)),
            pltpu.VMEM((n_tok, features), bf16),
            pltpu.VMEM((3, features, width), bf16),
            pltpu.VMEM((n_tok, width), bf16),
            pltpu.VMEM((n_tok, width), bf16),
            pltpu.VMEM((n_tok, width), bf16),
            pltpu.VMEM((n_tok, width), bf16),
            pltpu.VMEM((n_blocks, mine, dim, dim), f32),
            pltpu.VMEM((mine, dim, dim), f32),
            pltpu.VMEM((n_ctx // 2, mine, dim, dim), f32),
            pltpu.VMEM((n_blocks, mine, dim, dim), bf16),
            dma, dma, dma,
            dma((n_x, 2)), dma((n_x, 2)), dma((n_x, 2)), dma((n_x, 2)),
            dma((3 * cuts, n_ctx)), dma((3 * cuts, n_ctx)),
            dma((3 * cuts, n_ctx)), dma((3 * cuts, n_ctx)),
            dma((n_ctx // 2,)), dma((n_ctx // 2,)),
            dma((n_head,)), dma((n_head,)), dma((n_head,)), dma((n_head,)), dma,
        ],
        compiler_params=pltpu.CompilerParams(
            collective_id=0, has_side_effects=True, vmem_limit_bytes=60 * 1024 * 1024
        ),
    )(
        tokens,
        in_gain.reshape(1, features),
        projections,
        prior_state,
        out_gain.reshape(heads_here, 1, dim),
    )


def solution(mesh):
    in_specs = (
        P(("runs", "ctx", "head"), None),
        P(),
        P(None, "ctx", "head"),
        P(("runs", "head"), None, None),
        P("head"),
    )
    out_specs = P(("runs", "ctx", "head"), None)
    return jax.shard_map(
        functools.partial(on_device, mesh.shape["ctx"], mesh.shape["head"]),
        mesh=mesh, in_specs=in_specs, out_specs=out_specs, check_vma=False,
    )
```

```python
import functools

import jax
import jax.numpy as jnp
from jax import lax
from jax.experimental import pallas as pl
from jax.experimental.pallas import tpu as pltpu
from jax.sharding import PartitionSpec as P

BLOCK = 512
CORES = 2
MESH = pl.DeviceIdType.MESH
QUERY, KEY, VALUE = 0, 1, 2
AHEAD = 6
AT_PARTNER, AT_FIRST, AT_SECOND, AT_KEYS, AT_VALUES = 2, 3, 9, 10, 11


def dot(a, b, contract=((1,), (0,))):
    return lax.dot_general(a, b, (contract, ((), ())), preferred_element_type=jnp.float32)


def kernel(
    n_ctx, n_head,
    tok_hbm, gain_hbm, w_ref, prior_hbm, og_hbm,
    out_ref,
    tok_ref, gain_ref, prior_ref, og_ref, in_sems,
    x_buf, w_buf, q_buf, k_buf, v_buf, att, sums, totals, others, starts,
    own_sem, tz_send, tz_recv, tx_send, tx_recv, tc_send, tc_recv,
    wz_send, wz_recv, wy_send, wy_recv, st_send, st_recv, oz_send, oz_recv, o_send, o_recv, o_own,
):
    run = lax.axis_index("runs")
    z = lax.axis_index("ctx")
    h = lax.axis_index("head")
    n_x = n_head // CORES
    x, core = h // CORES, h % CORES
    half = z % 2
    partner = z + 1 - 2 * half
    rows_here = tok_ref.shape[0]
    rows = w_ref.shape[1]
    rows_half = rows // 2
    cuts = wz_send.shape[0] // 3
    rows_cut = rows_half // cuts
    stages = [(j, cut) for j in (KEY, VALUE, QUERY) for cut in range(cuts)]
    mine = prior_ref.shape[0]
    dim = prior_ref.shape[1]
    width = mine * dim
    n_tok = x_buf.shape[0]
    span = n_tok // 2
    n_blocks = n_tok // BLOCK
    n_pairs = n_ctx // 2
    other_run = {"runs": 1 - run}

    def slot(side, head):
        return pl.ds(pl.multiple_of((side * n_head + head) * rows_here, rows_here), rows_here)

    def cols(side):
        return pl.ds(pl.multiple_of(side * width, width), width)

    def w_rows(source, part, cut):
        start = pl.multiple_of(source * rows + part * rows_half + cut * rows_cut, rows_cut)
        return pl.ds(start, rows_cut)

    own_w = pltpu.make_async_copy(
        w_ref.at[:, :, cols(half)],
        w_buf.at[:, pl.ds(pl.multiple_of(z * rows, rows), rows), :],
        own_sem,
    )
    my_heads = pl.ds(half * mine, mine)
    loads = [
        pltpu.make_async_copy(src, dst, in_sems.at[n])
        for n, (src, dst) in enumerate((
            (tok_hbm, tok_ref), (gain_hbm, gain_ref),
            (prior_hbm.at[my_heads], prior_ref), (og_hbm.at[my_heads], og_ref),
        ))
    ]
    for load in loads:
        load.start()
    own_w.start()

    barrier = pltpu.get_barrier_semaphore()
    greeted = [other_run]
    greeted += [{"ctx": (z + k) % n_ctx} for k in range(1, n_ctx)]
    greeted += [{"head": (h + k) % n_head} for k in range(1, n_head)]
    greeted += [{"ctx": partner, "head": (h + k) % n_head} for k in range(1, n_head)]
    for device in greeted:
        pl.semaphore_signal(barrier, inc=1, device_id=device, device_id_type=MESH)

    loads[0].wait()
    loads[1].wait()
    wide = tok_ref[...].astype(jnp.float32)
    scale = lax.rsqrt(jnp.mean(wide * wide, axis=-1, keepdims=True) + 1e-06)
    x_buf[slot(half, h), :] = (wide * scale * gain_ref[...]).astype(jnp.bfloat16)
    pl.semaphore_wait(barrier, len(greeted))

    sent = []

    def send(src, dst, send_sem, recv_sem, device):
        copy = pltpu.make_async_remote_copy(
            src_ref=src, dst_ref=dst, send_sem=send_sem, recv_sem=recv_sem,
            device_id=device, device_id_type=MESH,
        )
        copy.start()
        sent.append(copy)

    def arrived(dst, send_sem, recv_sem):
        pltpu.make_async_remote_copy(
            src_ref=dst, dst_ref=dst, send_sem=send_sem, recv_sem=recv_sem,
            device_id=other_run, device_id_type=MESH,
        ).wait_recv()

    def spread(side, b):
        block = x_buf.at[slot(side, h), :]
        for d in range(1, n_x):
            send(block, block, tx_send.at[d, b], tx_recv.at[d, b],
                 {"head": ((x + d) % n_x) * CORES + core})
        send(block, block, tc_send.at[0, b], tc_recv.at[0, b],
             {"head": x * CORES + 1 - core})

    def pass_on(side, b):
        for d in range(1, n_x):
            head = ((x + n_x - d) % n_x) * CORES + core
            block = x_buf.at[slot(side, head), :]
            arrived(block, tx_send.at[d, b], tx_recv.at[d, b])
            send(block, block, tc_send.at[d, b], tc_recv.at[d, b],
                 {"head": x * CORES + 1 - core})

    def send_weights(stage):
        j, cut = stages[stage]
        for k in range(1, n_ctx):
            to = (z + k) % n_ctx
            start = pl.multiple_of(run * rows_half + cut * rows_cut, rows_cut)
            send(w_ref.at[j, pl.ds(start, rows_cut), cols(to % 2)],
                 w_buf.at[j, w_rows(z, run, cut), :],
                 wz_send.at[stage, k], wz_recv.at[stage, k], {"ctx": to})

    def swap_weights(stage):
        j, cut = stages[stage]
        for k in range(1, n_ctx):
            piece = w_buf.at[j, w_rows((z + n_ctx - k) % n_ctx, run, cut), :]
            arrived(piece, wz_send.at[stage, k], wz_recv.at[stage, k])
            send(piece, piece, wy_send.at[stage, k], wy_recv.at[stage, k], other_run)

    def wait_weights(matrix):
        for stage, (j, cut) in enumerate(stages):
            if j != matrix:
                continue
            for k in range(1, n_ctx):
                piece = w_buf.at[j, w_rows((z + n_ctx - k) % n_ctx, 1 - run, cut), :]
                arrived(piece, wy_send.at[stage, k], wy_recv.at[stage, k])

    def project(j, to):
        def tile(step, carry):
            at = pl.ds(pl.multiple_of(step * 256, 256), 256)
            to[at, :] = dot(x_buf[at, :], w_buf[j]).astype(jnp.bfloat16)
            return carry

        lax.fori_loop(0, n_tok // 256, tile, 0)

    def start_tokens():
        block = x_buf.at[slot(half, h), :]
        send(block, block, tz_send, tz_recv, {"ctx": partner})
        spread(half, 0)

    def partner_tokens():
        arrived(x_buf.at[slot(1 - half, h), :], tz_send, tz_recv)
        spread(1 - half, 1)

    def wait_tokens():
        for d in range(n_x):
            head = ((x + n_x - d) % n_x) * CORES + 1 - core
            for b, side in ((0, half), (1, 1 - half)):
                arrived(x_buf.at[slot(side, head), :], tc_send.at[d, b], tc_recv.at[d, b])

    def do_keys():
        wait_weights(KEY)
        project(KEY, k_buf)

    def do_values():
        wait_weights(VALUE)
        project(VALUE, v_buf)

    def do_sums():
        for i in range(mine):
            at = pl.ds(i * dim, dim)
            total = None
            for b in range(n_blocks):
                here = pl.ds(b * BLOCK, BLOCK)
                one = dot(k_buf[here, at], v_buf[here, at], ((0,), (0,)))
                sums[b, i] = one
                total = one if total is None else total + one
            totals[i] = total
        for k in range(1, n_pairs):
            send(totals, others.at[k], st_send.at[k], st_recv.at[k],
                 {"ctx": (z + 2 * k) % n_ctx})

    def do_starts():
        for k in range(1, n_pairs):
            arrived(others.at[k], st_send.at[k], st_recv.at[k])
        for i in range(mine):
            state = prior_ref[i]
            for k in range(1, n_pairs):
                state = state + jnp.where(z >= 2 * k, others[k, i], 0.0)
            for b in range(n_blocks):
                starts[b, i] = state.astype(jnp.bfloat16)
                state = state + sums[b, i]

    n_stages = len(stages)
    ahead = min(AHEAD * cuts // 4, n_stages)
    between = [[] for _ in range(n_stages + 1)]
    for at, work in (
        (AT_PARTNER, (partner_tokens,)),
        (AT_FIRST, (functools.partial(pass_on, half, 0),)),
        (AT_SECOND, (functools.partial(pass_on, 1 - half, 1),)),
        (AT_KEYS, (wait_tokens, own_w.wait, loads[2].wait, loads[3].wait, do_keys)),
        (AT_VALUES, (do_values, do_sums)),
    ):
        between[at * cuts // 4] += work
    start_tokens()
    for stage in range(ahead):
        send_weights(stage)
    for stage in range(n_stages):
        for work in between[stage]:
            work()
        swap_weights(stage)
        if stage + ahead < n_stages:
            send_weights(stage + ahead)
    for work in between[n_stages]:
        work()
    do_starts()
    wait_weights(QUERY)
    project(QUERY, q_buf)

    step_rows = 256
    out_cols = pl.ds(pl.multiple_of((h * 2 + half) * width, width), width)
    per_span = span // BLOCK

    def attend(side, bb, r):
        b = side * per_span + bb
        base = pl.multiple_of(b * BLOCK, BLOCK)
        seen = r + step_rows
        here = pl.ds(pl.multiple_of(base + r, step_rows), step_rows)
        before = pl.ds(base, seen)
        row = lax.broadcasted_iota(jnp.int32, (step_rows, seen), 0) + r
        col = lax.broadcasted_iota(jnp.int32, (step_rows, seen), 1)
        for i in range(mine):
            at = pl.ds(i * dim, dim)
            query = q_buf[here, at]
            scores = dot(query, k_buf[before, at], ((1,), (1,)))
            scores = jnp.where(row >= col, scores, 0.0).astype(jnp.bfloat16)
            mixed = dot(scores, v_buf[before, at]) + dot(query, starts[b, i])
            level = lax.rsqrt(jnp.mean(mixed * mixed, axis=-1, keepdims=True) + 1e-06)
            att[here, at] = (mixed * level * og_ref[i]).astype(jnp.bfloat16)

    for bb in range(per_span):
        for r in range(0, BLOCK, step_rows):
            attend(1 - half, bb, r)
            first = (bb * BLOCK + r) // rows_here
            for head in range(first, first + step_rows // rows_here):
                send(att.at[slot(1 - half, head), :], out_ref.at[:, out_cols],
                     oz_send.at[head], oz_recv.at[h], {"ctx": partner, "head": head})
    for bb in range(per_span):
        for r in range(0, BLOCK, step_rows):
            attend(half, bb, r)
    for dh in range(1, n_head):
        send(att.at[slot(half, (h + dh) % n_head), :], out_ref.at[:, out_cols],
             o_send.at[dh], o_recv.at[dh], {"head": (h + dh) % n_head})
    own_out = pltpu.make_async_copy(att.at[slot(half, h), :], out_ref.at[:, out_cols], o_own)
    own_out.start()

    def out_place(head, side):
        return out_ref.at[:, pl.ds(pl.multiple_of((head * 2 + side) * width, width), width)]

    for head in range(n_head):
        arrived(out_place(head, 1 - half), oz_send.at[head], oz_recv.at[head])
    for dh in range(1, n_head):
        arrived(out_place((h + n_head - dh) % n_head, half), o_send.at[dh], o_recv.at[dh])
    own_out.wait()
    for copy in sent:
        copy.wait_send()


def on_device(n_ctx, n_head, tokens, in_gain, projections, prior_state, out_gain):
    rows_here, features = tokens.shape
    heads_here, dim, _ = prior_state.shape
    mine = heads_here // 2
    width = mine * dim
    n_tok = 2 * n_head * rows_here
    n_blocks = n_tok // BLOCK
    n_x = n_head // CORES
    cuts = min(4, projections.shape[1] // 32)
    dma = pltpu.SemaphoreType.DMA
    vmem = pl.BlockSpec(memory_space=pltpu.VMEM)
    bf16, f32 = jnp.bfloat16, jnp.float32
    return pl.pallas_call(
        functools.partial(kernel, n_ctx, n_head),
        out_shape=jax.ShapeDtypeStruct((rows_here, features), bf16),
        in_specs=[pl.BlockSpec(memory_space=pltpu.HBM)] * 5,
        out_specs=vmem,
        scratch_shapes=[
            pltpu.VMEM((rows_here, features), bf16),
            pltpu.VMEM((1, features), f32),
            pltpu.VMEM((mine, dim, dim), f32),
            pltpu.VMEM((mine, 1, dim), f32),
            dma((4,)),
            pltpu.VMEM((n_tok, features), bf16),
            pltpu.VMEM((3, features, width), bf16),
            pltpu.VMEM((n_tok, width), bf16),
            pltpu.VMEM((n_tok, width), bf16),
            pltpu.VMEM((n_tok, width), bf16),
            pltpu.VMEM((n_tok, width), bf16),
            pltpu.VMEM((n_blocks, mine, dim, dim), f32),
            pltpu.VMEM((mine, dim, dim), f32),
            pltpu.VMEM((n_ctx // 2, mine, dim, dim), f32),
            pltpu.VMEM((n_blocks, mine, dim, dim), bf16),
            dma, dma, dma,
            dma((n_x, 2)), dma((n_x, 2)), dma((n_x, 2)), dma((n_x, 2)),
            dma((3 * cuts, n_ctx)), dma((3 * cuts, n_ctx)),
            dma((3 * cuts, n_ctx)), dma((3 * cuts, n_ctx)),
            dma((n_ctx // 2,)), dma((n_ctx // 2,)),
            dma((n_head,)), dma((n_head,)), dma((n_head,)), dma((n_head,)), dma,
        ],
        compiler_params=pltpu.CompilerParams(
            collective_id=0, has_side_effects=True, vmem_limit_bytes=60 * 1024 * 1024
        ),
    )(
        tokens,
        in_gain.reshape(1, features),
        projections,
        prior_state,
        out_gain.reshape(heads_here, 1, dim),
    )


def solution(mesh):
    in_specs = (
        P(("runs", "ctx", "head"), None),
        P(),
        P(None, "ctx", "head"),
        P(("runs", "head"), None, None),
        P("head"),
    )
    out_specs = P(("runs", "ctx", "head"), None)
    return jax.shard_map(
        functools.partial(on_device, mesh.shape["ctx"], mesh.shape["head"]),
        mesh=mesh, in_specs=in_specs, out_specs=out_specs, check_vma=False,
    )
```
